32 devices in a mesh: seq: 8 (over z, core), head: 4 (over y, x).
Axes of the slice: x: 2, y: 2, z: 4, core: 2. Of those that a mesh axis runs over, the one named last changes fastest.
Arguments:
- grad_output: bfloat16 [8192, 4096], P('seq', 'head'), may hold values from -6 to 6
- out_weight: bfloat16 [4096, 8192], P('seq', 'head'), may hold values from -0.0625 to 0.0625
- ssd_out: bfloat16 [8192, 8192], P('seq', 'head'), may hold values from -520 to 520
- gate: bfloat16 [8192, 8192], P('seq', 'head'), may hold values from -5 to 5
- norm_weight: float32 [8192], P('head'), may hold values from 0.5 to 1.5
- time_step: float32 [128, 8192], P('head', 'seq'), may hold values from 0.01 to 0.1
- log_decay: float32 [128, 8192], P('head', 'seq'), may hold values from -0.7 to 0
- state_in: bfloat16 [8192, 8, 128], P('seq'), may hold values from -1.796875 to 1.796875
- state_out: bfloat16 [8192, 8, 128], P('seq'), may hold values from -1.796875 to 1.796875
- skip: float32 [128], P('head'), may hold values from 0.5 to 1.5
Outputs:
- grad_x: bfloat16 [8192, 8192], P('seq', 'head')
- grad_gate: bfloat16 [8192, 8192], P('seq', 'head')
- grad_out_weight: float32 [4096, 8192], P('seq', 'head')
The draws below stay inside these ranges and needn't reach their ends.
All inputs are finite; a program needn't handle non-finite values.
Results may differ from the reference program's by a relative error of at most 0.014.
Values may be sent and summed in bfloat16 or wider, within the bound.
A program may use at most 192 MiB of HBM per device.

```python
import math
from functools import partial
import jax
import jax.numpy as jnp
from jax import lax

D = 4096
HEADS = 128
HDIM = 64
NSTATE = 128
GROUPS = 8
BLOCK_LEN = 256
TOK_DEV = 1024
TOKENS = 8192
DI = 8192


def draw_log_decay(key, part):
    keys = jax.random.split(jax.random.fold_in(key, 11), 7)
    order = jax.random.permutation(keys[0], HEADS)
    slow_count = HEADS // 2
    slow_heads = order < slow_count
    chain = float(TOKENS)
    slow_rate = jnp.exp(jax.random.uniform(keys[1], (HEADS,), jnp.float32, math.log(0.1 / chain), math.log(0.5 / chain)))
    fast_rate = jnp.exp(jax.random.uniform(keys[2], (HEADS,), jnp.float32, math.log(2.0 / chain), math.log(0.035)))
    fading_speed = jnp.where(slow_heads, slow_rate, fast_rate)
    blocks = TOKENS // TOK_DEV
    multiplier_coefficient = jnp.exp2(jax.random.uniform(keys[3], (HEADS, blocks), jnp.float32, -1.0, 1.0))
    multiplier_coefficient = jnp.repeat(multiplier_coefficient, TOK_DEV, axis=1)
    approximate_guess = jax.random.uniform(keys[4], (HEADS, TOKENS), jnp.float32, 0.5, 1.5)
    seat_locations = jax.random.randint(keys[5], (3,), 0, TOKENS)
    increment_lengths = jax.random.uniform(keys[6], (3,), jnp.float32, 0.22, 0.51)
    sequence_indices = jnp.arange(TOKENS)
    clustered_spans = jnp.max(jnp.where(sequence_indices[None, :] == seat_locations[:, None], increment_lengths[:, None], 0.0), axis=0)
    return (-(fading_speed[:, None] * multiplier_coefficient * approximate_guess) - clustered_spans[None, :]).astype(jnp.float32)


def draw_ssd_out(key, part):
    keys = jax.random.split(jax.random.fold_in(key, 23), 4)
    row_scale = jnp.exp(jax.random.uniform(keys[0], (TOKENS,), jnp.float32, 0.0, math.log(10.0)))
    column_scale = jnp.exp(jax.random.uniform(keys[1], (DI,), jnp.float32, math.log(0.3), math.log(3.0)))
    ramp = jnp.arange(DI, dtype=jnp.float32) / DI
    base = jax.random.truncated_normal(keys[3], -4.0, 4.0, (TOKENS, DI), jnp.float32)
    rising = jnp.power(3.0, 0.5 * ramp)
    return (base * row_scale[:, None] * (column_scale * rising)[None, :]).astype(jnp.bfloat16)


def spiked(entries, key, source, target, parts, factor):
    def block_of(dim):
        return (jnp.arange(entries.shape[dim]) // (entries.shape[dim] // parts)).reshape((-1,) + (1,) * (entries.ndim - 1 - dim))

    one_side = jax.random.permutation(key, parts)[block_of(target)]
    other_side = (block_of(target) + parts // 2) % parts
    return jnp.where((block_of(source) == one_side) | (block_of(source) == other_side), factor * entries, entries)


def block_scale(own_key, extent, pieces, low, high):
    def one(dim, blocks):
        steps = jax.random.uniform(jax.random.fold_in(jax.random.fold_in(own_key, 6), dim), (blocks,), jnp.float32, low / len(pieces), high / len(pieces))
        return jnp.repeat(jnp.exp(steps), extent[dim] // blocks).reshape((-1,) + (1,) * (len(extent) - dim - 1))

    level = one(*pieces[0])
    for cut in pieces[1:]:
        level = level * one(*cut)
    return level


def gaussian(own_key, shape, scale, most, shards=(), held_as=jnp.bfloat16):
    loudness = block_scale(own_key, shape, shards, -0.22, 0.18) if shards else 1.0
    drawn = jax.random.normal(own_key, shape, jnp.float32) * scale * loudness
    return jnp.minimum(jnp.maximum(drawn, -most), most).astype(held_as)


def heavy_noise(stream_key, extent, width, bound, cuts, heavy, kind=jnp.bfloat16):
    drawn = width * jax.random.normal(stream_key, extent, jnp.float32)
    if cuts:
        drawn = drawn * block_scale(stream_key, extent, cuts, -0.22, 0.18)
    return jnp.clip(spiked(drawn, jax.random.fold_in(stream_key, 3), *heavy), -bound, bound).astype(kind)


def setup_inputs(seed: int = 0) -> dict:
    seeds = jax.random.split(jax.random.key(seed), 11)
    return {
        "grad_output": heavy_noise(seeds[0], (TOKENS, D), 1.0, 6.0, ((0, 8), (1, 4)), (0, 1, 8, 2.0)),
        "out_weight": gaussian(seeds[1], (D, DI), DI ** -0.5, 0.0625, ((0, 8), (1, 4))),
        "ssd_out": draw_ssd_out(jax.random.fold_in(seeds[10], 71), 0),
        "gate": gaussian(seeds[3], (TOKENS, DI), 1.0, 5.0, ((0, 8), (1, 4))),
        "norm_weight": jnp.clip(1.0 + 0.1 * jax.random.normal(seeds[4], (DI,), jnp.float32), 0.5, 1.5),
        "time_step": jnp.clip(jnp.exp(math.log(0.1) - 2.3025851 * jax.random.uniform(seeds[5], (HEADS, TOKENS), jnp.float32) ** block_scale(seeds[5], (HEADS, TOKENS), ((0, 4), (1, 8)), -0.2, 0.2)), 0.01, 0.1),
        "log_decay": draw_log_decay(jax.random.fold_in(seeds[10], 71), 0),
        "state_in": gaussian(seeds[7], (TOKENS, GROUPS, NSTATE), 0.3, 1.796875, ((0, 8),)),
        "state_out": gaussian(seeds[8], (TOKENS, GROUPS, NSTATE), 0.3, 1.796875, ((0, 8),)),
        "skip": jnp.clip(0.5 + 1.0 * jax.random.uniform(seeds[9], (HEADS,), jnp.float32) ** block_scale(seeds[9], (HEADS,), ((0, 4),), -0.2, 0.2), 0.5, 1.5),
    }


epsilon = 1e-05

def head_grad(head, grad_ssd, time_step, log_decay, state_in, state_out, skip):
    group = (head // (HEADS // GROUPS)).astype(jnp.int32)
    blocks = TOKENS // BLOCK_LEN
    start_col = (head * HDIM).astype(jnp.int32)
    grad_cols = lax.dynamic_slice_in_dim(grad_ssd, start_col, HDIM, 1).astype(jnp.float32)
    grad_cols = grad_cols.reshape(blocks, BLOCK_LEN, HDIM)
    b_rows = lax.dynamic_index_in_dim(state_in, group, 1, keepdims=False).astype(jnp.float32)
    b_rows = b_rows.reshape(blocks, BLOCK_LEN, NSTATE)
    c_rows = lax.dynamic_index_in_dim(state_out, group, 1, keepdims=False).astype(jnp.float32)
    c_rows = c_rows.reshape(blocks, BLOCK_LEN, NSTATE)
    rates = lax.dynamic_index_in_dim(log_decay, head, 0, keepdims=False).reshape(blocks, BLOCK_LEN)
    step_sizes = lax.dynamic_index_in_dim(time_step, head, 0, keepdims=False).reshape(blocks, BLOCK_LEN)
    skip_head = lax.dynamic_index_in_dim(skip, head, 0, keepdims=False)
    cumulative = jnp.cumsum(rates, axis=1)
    block_total = cumulative[:, -1]
    sequence_indices = jnp.arange(BLOCK_LEN)
    upper_mask = sequence_indices[None, :] >= sequence_indices[:, None]
    scores = jnp.einsum('ktn,ksn->kts', b_rows, c_rows)
    log_gap = cumulative[:, None, :] - cumulative[:, :, None]
    block_weights = jnp.where(upper_mask, scores * jnp.exp(jnp.minimum(log_gap, 0.0)), 0.0).astype(jnp.bfloat16)
    block_weights = lax.optimization_barrier(block_weights).astype(jnp.float32)
    within = jnp.einsum('kts,ksp->ktp', block_weights, grad_cols)
    scaled = (jnp.exp(cumulative)[:, :, None] * grad_cols).astype(jnp.bfloat16)
    scaled = lax.optimization_barrier(scaled).astype(jnp.float32)
    block_state = jnp.einsum('ksp,ksn->kpn', scaled, c_rows)

    def fold_block(carried, inputs):
        state_now, total_now = inputs
        return (state_now + jnp.exp(total_now) * carried, carried)
    unused, carry = lax.scan(fold_block, jnp.zeros((HDIM, NSTATE), jnp.float32), (block_state, block_total), reverse=True)
    carry_low = lax.optimization_barrier(carry.astype(jnp.bfloat16)).astype(jnp.float32)
    across = jnp.einsum('kpn,ktn->ktp', carry_low, b_rows) * jnp.exp(block_total[:, None] - cumulative)[:, :, None]
    result = step_sizes[:, :, None] * (within + across) + skip_head * grad_cols
    return result.reshape(TOKENS, HDIM).astype(jnp.bfloat16)

def reference(grad_output, out_weight, ssd_out, gate, norm_weight, time_step, log_decay, state_in, state_out, skip):
    values = ssd_out.astype(jnp.float32)
    gate_values = gate.astype(jnp.float32)
    sigmoid_gate = jax.nn.sigmoid(gate_values)
    silu_gate = gate_values * sigmoid_gate
    gated_values = values * silu_gate
    inverse_rms = lax.rsqrt(lax.optimization_barrier(jnp.mean(gated_values * gated_values, axis=1, keepdims=True)) + epsilon)
    normed = (gated_values * inverse_rms * norm_weight).astype(jnp.bfloat16)
    normed_grad = jnp.dot(grad_output, out_weight, preferred_element_type=jnp.float32)
    weighted = lax.optimization_barrier(jnp.sum(norm_weight * normed_grad * gated_values, axis=1, keepdims=True))
    gated_grad = inverse_rms * norm_weight * normed_grad - gated_values * inverse_rms ** 3 * weighted / DI
    grad_gate = (gated_grad * values * sigmoid_gate * (1.0 + gate_values * (1.0 - sigmoid_gate))).astype(jnp.bfloat16)
    grad_ssd = (gated_grad * silu_gate).astype(jnp.bfloat16)
    grad_out_weight = jnp.dot(grad_output.T, normed, preferred_element_type=jnp.float32) * (1.0 / math.sqrt(TOKENS))
    per_head = lax.map(partial(head_grad, grad_ssd=grad_ssd, time_step=time_step, log_decay=log_decay, state_in=state_in, state_out=state_out, skip=skip), jnp.arange(HEADS, dtype=jnp.int32))
    grad_x = jnp.transpose(per_head, (1, 0, 2)).reshape(TOKENS, DI)
    return (grad_x, grad_gate, grad_out_weight)
```

```python
import math

import jax
import jax.numpy as jnp
from jax import lax
from jax.sharding import PartitionSpec as P

HEADS = 128
GROUPS = 8
BLOCK_LEN = 256


epsilon = 1e-05


def shifted(x, axis, by):
    size = lax.axis_size(axis)
    pairs = [(i, i + by) for i in range(size) if 0 <= i + by < size]
    return lax.ppermute(x, axis, pairs)


def gather_columns(x, axis):
    size = lax.axis_size(axis)
    me = lax.axis_index(axis)
    width = x.shape[1]
    full = jnp.zeros((x.shape[0], width * size), x.dtype)
    full = lax.dynamic_update_slice(full, x, (0, me * width))
    for step in range(1, size):
        piece = lax.ppermute(x, axis, [(i, i ^ step) for i in range(size)])
        full = lax.dynamic_update_slice(full, piece, (0, (me ^ step) * width))
    return full


def arriving(summary, decay, axis):
    size = lax.axis_size(axis)

    def fetch(state, factor, by):
        return (
            shifted(state.astype(jnp.bfloat16), axis, -by).astype(jnp.float32),
            shifted(factor, axis, -by),
        )

    state, factor = fetch(summary, decay, 1)
    by = 1
    while by < size - 1:
        far_state, far_factor = fetch(state, factor, by)
        state = state + factor[:, None, None] * far_state
        factor = factor * far_factor
        by *= 2
    return state


def on_device(
    grad_output,
    out_weight,
    ssd_out,
    gate,
    norm_weight,
    time_step,
    log_decay,
    state_in,
    state_out,
    skip,
):
    tok_rows = ssd_out.shape[0]
    local_width = ssd_out.shape[1]
    total_width = local_width * lax.axis_size("head")
    full_weight = lax.all_gather(out_weight, "seq", axis=0, tiled=True)
    full_grad = gather_columns(grad_output, "head")
    values = ssd_out.astype(jnp.float32)
    gate_values = gate.astype(jnp.float32)
    sigmoid_gate = jax.nn.sigmoid(gate_values)
    silu_gate = gate_values * sigmoid_gate
    gated_values = values * silu_gate
    local_squares = jnp.sum(gated_values * gated_values, axis=1)
    squares = lax.psum(local_squares, "head")
    squares_here, full_weight = lax.optimization_barrier((squares, full_weight))
    normed_grad = jnp.dot(full_grad, full_weight, preferred_element_type=jnp.float32)
    weighted = lax.psum(jnp.sum(norm_weight * normed_grad * gated_values, axis=1), "head")
    inverse_rms = lax.rsqrt(squares[:, None] / total_width + epsilon)
    normed = (gated_values * inverse_rms * norm_weight).astype(jnp.bfloat16)
    gated_grad = (
        inverse_rms * norm_weight * normed_grad
        - gated_values * inverse_rms**3 * weighted[:, None] / total_width
    )
    grad_gate = (
        gated_grad * values * sigmoid_gate * (1.0 + gate_values * (1.0 - sigmoid_gate))
    ).astype(jnp.bfloat16)
    grad_ssd = (gated_grad * silu_gate).astype(jnp.bfloat16)
    partial_sum = lax.dot_general(
        full_grad, normed, (((0,), (0,)), ((), ())), preferred_element_type=jnp.float32
    ).astype(jnp.bfloat16)
    weight_sum = lax.psum_scatter(
        partial_sum, "seq", scatter_dimension=0, tiled=True
    ).astype(jnp.float32)
    grad_out_weight = weight_sum * (1.0 / math.sqrt(tok_rows * lax.axis_size("seq")))
    heads_here = time_step.shape[0]
    head_width = local_width // heads_here
    blocks = tok_rows // BLOCK_LEN
    state_width = state_in.shape[2]
    group_count = state_in.shape[1]
    first_head = lax.axis_index("head") * heads_here
    head_ids = first_head + jnp.arange(heads_here, dtype=jnp.int32)
    group_ids = head_ids // (HEADS // GROUPS)
    group_pick = (group_ids[:, None] == jnp.arange(group_count, dtype=jnp.int32)[None, :]).astype(
        jnp.bfloat16
    )
    b_heads = jnp.einsum(
        "tgn,hg->htn", state_in, group_pick, preferred_element_type=jnp.float32
    ).astype(jnp.bfloat16)
    b_heads = b_heads.reshape(heads_here, blocks, BLOCK_LEN, state_width)
    c_heads = jnp.einsum(
        "tgn,hg->htn", state_out, group_pick, preferred_element_type=jnp.float32
    ).astype(jnp.bfloat16)
    c_heads = c_heads.reshape(heads_here, blocks, BLOCK_LEN, state_width)
    grad_heads = grad_ssd.reshape(tok_rows, heads_here, head_width).transpose(1, 0, 2)
    grad_heads = grad_heads.reshape(heads_here, blocks, BLOCK_LEN, head_width)
    cumulative = jnp.cumsum(log_decay.reshape(heads_here, blocks, BLOCK_LEN), axis=2)
    block_total = cumulative[..., -1]
    sequence_indices = jnp.arange(BLOCK_LEN)
    upper_mask = sequence_indices[None, :] >= sequence_indices[:, None]
    scores = jnp.einsum("hktn,hksn->hkts", b_heads, c_heads, preferred_element_type=jnp.float32)
    log_gap = cumulative[..., None, :] - cumulative[..., :, None]
    block_weights = jnp.where(upper_mask, scores * jnp.exp(jnp.minimum(log_gap, 0.0)), 0.0).astype(
        jnp.bfloat16
    )
    within = jnp.einsum(
        "hkts,hksp->hktp", block_weights, grad_heads, preferred_element_type=jnp.float32
    )
    grad_float = grad_heads.astype(jnp.float32)
    scaled = (jnp.exp(cumulative)[..., None] * grad_float).astype(jnp.bfloat16)
    block_state = jnp.einsum("hksp,hksn->hkpn", scaled, c_heads, preferred_element_type=jnp.float32)

    def fold_block(carried, inputs):
        state_now, total_now = inputs
        return (state_now + jnp.exp(total_now)[:, None, None] * carried, carried)

    zero_state = jnp.zeros((heads_here, head_width, state_width), jnp.float32)
    summary, inside = lax.scan(
        fold_block, zero_state, (block_state.transpose(1, 0, 2, 3), block_total.T), reverse=True
    )
    decay_total = jnp.exp(jnp.sum(block_total, axis=1))
    tail_decay = jnp.exp(
        jnp.sum(block_total, axis=1, keepdims=True) - jnp.cumsum(block_total, axis=1)
    )

    remote = arriving(summary, decay_total, "seq")
    full_states = inside.transpose(1, 0, 2, 3) + tail_decay[..., None, None] * remote[:, None]
    carry_low = full_states.astype(jnp.bfloat16)
    across = jnp.einsum("hkpn,hktn->hktp", carry_low, b_heads, preferred_element_type=jnp.float32)
    across = across * jnp.exp(block_total[..., None] - cumulative)[..., None]
    step_sizes = time_step.reshape(heads_here, blocks, BLOCK_LEN)
    grad_head = step_sizes[..., None] * (within + across) + skip[:, None, None, None] * grad_float
    grad_x = (
        grad_head.reshape(heads_here, tok_rows, head_width)
        .transpose(1, 0, 2)
        .reshape(tok_rows, local_width)
    )
    return (grad_x.astype(jnp.bfloat16), grad_gate, grad_out_weight)


def solution(mesh):
    return jax.shard_map(
        on_device,
        mesh=mesh,
        in_specs=(
            P("seq", "head"),
            P("seq", "head"),
            P("seq", "head"),
            P("seq", "head"),
            P("head"),
            P("head", "seq"),
            P("head", "seq"),
            P("seq", None, None),
            P("seq", None, None),
            P("head"),
        ),
        out_specs=(P("seq", "head"), P("seq", "head"), P("seq", "head")),
        check_vma=False,
    )
```

```python
import math

import jax
import jax.numpy as jnp
from jax import lax
from jax.sharding import PartitionSpec as P

HEADS = 128
GROUPS = 8
BLOCK_LEN = 256


epsilon = 1e-05


def shifted(x, axis, by):
    size = lax.axis_size(axis)
    pairs = [(i, i + by) for i in range(size) if 0 <= i + by < size]
    return lax.ppermute(x, axis, pairs)


def gather_columns(x, axis):
    size = lax.axis_size(axis)
    me = lax.axis_index(axis)
    width = x.shape[1]
    full = jnp.zeros((x.shape[0], width * size), x.dtype)
    full = lax.dynamic_update_slice(full, x, (0, me * width))
    for step in range(1, size):
        piece = lax.ppermute(x, axis, [(i, i ^ step) for i in range(size)])
        full = lax.dynamic_update_slice(full, piece, (0, (me ^ step) * width))
    return full


def arriving(summary, totals, axis):
    size = lax.axis_size(axis)
    me = lax.axis_index(axis)
    pair_id, side = me // 2, me % 2
    first = side == 0
    half = summary.shape[0] // 2
    swap = [(i, i ^ 1) for i in range(size)]

    def partner(x):
        return lax.ppermute(x.astype(jnp.bfloat16), axis, swap).astype(jnp.float32)

    def mine(x):
        return lax.dynamic_slice_in_dim(x, side * half, half, 0)

    def decay(which):
        return jnp.exp(lax.dynamic_index_in_dim(totals, which, 0, keepdims=False))[:, None, None]

    other = partner(summary)
    lower = jnp.where(first, summary, other)
    upper = jnp.where(first, other, summary)
    pair = mine(lower + decay(2 * pair_id) * upper).astype(jnp.bfloat16)
    pair_totals = totals[0::2] + totals[1::2]
    order = jnp.arange(size // 2)[:, None]
    carry = jnp.zeros(pair.shape, jnp.float32)
    for hop in range(1, size // 2):
        between = (order > pair_id) & (order < pair_id + hop)
        weight = jnp.exp(jnp.sum(jnp.where(between, pair_totals, 0.0), axis=0))
        carry = carry + mine(weight)[:, None, None] * shifted(pair, axis, -2 * hop).astype(
            jnp.float32
        )
    swapped = partner(carry)
    whole = jnp.where(
        first, jnp.concatenate([carry, swapped]), jnp.concatenate([swapped, carry])
    )
    return jnp.where(first, upper + decay(2 * pair_id + 1) * whole, whole)


def on_device(
    grad_output,
    out_weight,
    ssd_out,
    gate,
    norm_weight,
    time_step,
    log_decay,
    state_in,
    state_out,
    skip,
):
    tok_rows = ssd_out.shape[0]
    local_width = ssd_out.shape[1]
    total_width = local_width * lax.axis_size("head")
    full_weight = lax.all_gather(out_weight, "seq", axis=0, tiled=True)
    full_grad = gather_columns(grad_output, "head")
    values = ssd_out.astype(jnp.float32)
    gate_values = gate.astype(jnp.float32)
    sigmoid_gate = jax.nn.sigmoid(gate_values)
    silu_gate = gate_values * sigmoid_gate
    gated_values = values * silu_gate
    local_squares = jnp.sum(gated_values * gated_values, axis=1)
    squares = lax.psum(local_squares, "head")
    totals = lax.all_gather(jnp.sum(log_decay, axis=1), "seq", axis=0)
    squares_here, full_weight, totals = lax.optimization_barrier((squares, full_weight, totals))
    normed_grad = jnp.dot(full_grad, full_weight, preferred_element_type=jnp.float32)
    weighted = lax.psum(jnp.sum(norm_weight * normed_grad * gated_values, axis=1), "head")
    inverse_rms = lax.rsqrt(squares[:, None] / total_width + epsilon)
    normed = (gated_values * inverse_rms * norm_weight).astype(jnp.bfloat16)
    gated_grad = (
        inverse_rms * norm_weight * normed_grad
        - gated_values * inverse_rms**3 * weighted[:, None] / total_width
    )
    grad_gate = (
        gated_grad * values * sigmoid_gate * (1.0 + gate_values * (1.0 - sigmoid_gate))
    ).astype(jnp.bfloat16)
    grad_ssd = (gated_grad * silu_gate).astype(jnp.bfloat16)
    partial_sum = lax.dot_general(
        full_grad, normed, (((0,), (0,)), ((), ())), preferred_element_type=jnp.float32
    ).astype(jnp.bfloat16)
    weight_sum = lax.psum_scatter(
        partial_sum, "seq", scatter_dimension=0, tiled=True
    ).astype(jnp.float32)
    grad_out_weight = weight_sum * (1.0 / math.sqrt(tok_rows * lax.axis_size("seq")))
    heads_here = time_step.shape[0]
    head_width = local_width // heads_here
    blocks = tok_rows // BLOCK_LEN
    state_width = state_in.shape[2]
    group_count = state_in.shape[1]
    first_head = lax.axis_index("head") * heads_here
    head_ids = first_head + jnp.arange(heads_here, dtype=jnp.int32)
    group_ids = head_ids // (HEADS // GROUPS)
    group_pick = (group_ids[:, None] == jnp.arange(group_count, dtype=jnp.int32)[None, :]).astype(
        jnp.bfloat16
    )
    b_heads = jnp.einsum(
        "tgn,hg->htn", state_in, group_pick, preferred_element_type=jnp.float32
    ).astype(jnp.bfloat16)
    b_heads = b_heads.reshape(heads_here, blocks, BLOCK_LEN, state_width)
    c_heads = jnp.einsum(
        "tgn,hg->htn", state_out, group_pick, preferred_element_type=jnp.float32
    ).astype(jnp.bfloat16)
    c_heads = c_heads.reshape(heads_here, blocks, BLOCK_LEN, state_width)
    grad_heads = grad_ssd.reshape(tok_rows, heads_here, head_width).transpose(1, 0, 2)
    grad_heads = grad_heads.reshape(heads_here, blocks, BLOCK_LEN, head_width)
    cumulative = jnp.cumsum(log_decay.reshape(heads_here, blocks, BLOCK_LEN), axis=2)
    block_total = cumulative[..., -1]
    sequence_indices = jnp.arange(BLOCK_LEN)
    upper_mask = sequence_indices[None, :] >= sequence_indices[:, None]
    scores = jnp.einsum("hktn,hksn->hkts", b_heads, c_heads, preferred_element_type=jnp.float32)
    log_gap = cumulative[..., None, :] - cumulative[..., :, None]
    block_weights = jnp.where(upper_mask, scores * jnp.exp(jnp.minimum(log_gap, 0.0)), 0.0).astype(
        jnp.bfloat16
    )
    within = jnp.einsum(
        "hkts,hksp->hktp", block_weights, grad_heads, preferred_element_type=jnp.float32
    )
    within = lax.optimization_barrier(within)
    grad_float = grad_heads.astype(jnp.float32)
    scaled = (jnp.exp(cumulative)[..., None] * grad_float).astype(jnp.bfloat16)
    block_state = jnp.einsum("hksp,hksn->hkpn", scaled, c_heads, preferred_element_type=jnp.float32)

    def fold_block(carried, inputs):
        state_now, total_now = inputs
        return (state_now + jnp.exp(total_now)[:, None, None] * carried, carried)

    zero_state = jnp.zeros((heads_here, head_width, state_width), jnp.float32)
    summary, inside = lax.scan(
        fold_block, zero_state, (block_state.transpose(1, 0, 2, 3), block_total.T), reverse=True
    )
    tail_decay = jnp.exp(
        jnp.sum(block_total, axis=1, keepdims=True) - jnp.cumsum(block_total, axis=1)
    )

    remote = arriving(summary, totals, "seq")
    full_states = inside.transpose(1, 0, 2, 3) + tail_decay[..., None, None] * remote[:, None]
    carry_low = full_states.astype(jnp.bfloat16)
    across = jnp.einsum("hkpn,hktn->hktp", carry_low, b_heads, preferred_element_type=jnp.float32)
    across = across * jnp.exp(block_total[..., None] - cumulative)[..., None]
    step_sizes = time_step.reshape(heads_here, blocks, BLOCK_LEN)
    grad_head = step_sizes[..., None] * (within + across) + skip[:, None, None, None] * grad_float
    grad_x = (
        grad_head.reshape(heads_here, tok_rows, head_width)
        .transpose(1, 0, 2)
        .reshape(tok_rows, local_width)
    )
    return (grad_x.astype(jnp.bfloat16), grad_gate, grad_out_weight)


def solution(mesh):
    return jax.shard_map(
        on_device,
        mesh=mesh,
        in_specs=(
            P("seq", "head"),
            P("seq", "head"),
            P("seq", "head"),
            P("seq", "head"),
            P("head"),
            P("head", "seq"),
            P("head", "seq"),
            P("seq", None, None),
            P("seq", None, None),
            P("head"),
        ),
        out_specs=(P("seq", "head"), P("seq", "head"), P("seq", "head")),
        check_vma=False,
    )
```
